32 devices in a mesh: seq: 8 (over z, y), mp: 4 (over x, core).
Axes of the slice: x: 2, y: 2, z: 4, core: 2. Of those that a mesh axis runs over, the one named last changes fastest.
Arguments:
- block_input: bfloat16 [1, 1280, 2560], P(None, 'seq'), may hold values from -6 to 6
- mix_gain: float32 [2560], replicated, may hold values from 0.5 to 1.5
- x_weight: bfloat16 [2560, 2560], P(None, 'mp'), may hold values from -0.125 to 0.125
- y_weight: bfloat16 [2560, 2560], P(None, 'mp'), may hold values from -0.125 to 0.125
- conv_weight: float32 [4, 2560], P(None, 'mp'), may hold values from -3 to 3
- conv_bias: float32 [2560], P('mp'), may hold values from -3 to 3
- input_gate: bfloat16 [256, 2560], P(None, 'mp'), may hold values from -0.375 to 0.375
- decay_gate: bfloat16 [256, 2560], P(None, 'mp'), may hold values from -0.375 to 0.375
- decay_param: float32 [2560], P('mp'), may hold values from -13 to -5
- out_weight: bfloat16 [2560, 2560], P('mp'), may hold values from -0.125 to 0.125
- ffn_gain: float32 [2560], replicated, may hold values from 0.5 to 1.5
- gate_weight: bfloat16 [2560, 7680], P(None, 'mp'), may hold values from -0.125 to 0.125
- up_weight: bfloat16 [2560, 7680], P(None, 'mp'), may hold values from -0.125 to 0.125
- down_weight: bfloat16 [7680, 2560], P('mp'), may hold values from -0.0625 to 0.0625
- out_cotangent: bfloat16 [1, 1280, 2560], P(None, 'seq'), may hold values from -6 to 6
Outputs:
- block_output: bfloat16 [1, 1280, 2560], P(None, 'seq')
- input_grad: bfloat16 [1, 1280, 2560], P(None, 'seq')
- mix_gain_grad: float32 [2560], P('seq')
- x_weight_grad: float32 [2560, 2560], P('seq', 'mp')
- y_weight_grad: float32 [2560, 2560], P('seq', 'mp')
- conv_weight_grad: float32 [4, 2560], P(None, ('mp', 'seq'))
- conv_bias_grad: float32 [2560], P(('mp', 'seq'))
- input_gate_grad: float32 [256, 2560], P('seq', 'mp')
- decay_gate_grad: float32 [256, 2560], P('seq', 'mp')
- decay_param_grad: float32 [2560], P(('mp', 'seq'))
- out_weight_grad: float32 [2560, 2560], P('mp', 'seq')
- ffn_gain_grad: float32 [2560], P('seq')
- gate_weight_grad: float32 [2560, 7680], P('seq', 'mp')
- up_weight_grad: float32 [2560, 7680], P('seq', 'mp')
- down_weight_grad: float32 [7680, 2560], P('mp', 'seq')
The draws below stay inside these ranges and needn't reach their ends.
All inputs are finite; a program needn't handle non-finite values.
Results may differ from the reference program's by a relative error of at most 0.009.
Values may be sent and summed in bfloat16 or wider, within the bound.
No kernel may reach another device: no remote copies, remote signals or barrier semaphores. Data moves between devices by JAX's collectives and lax.ppermute only.
A program may use at most 320 MiB of HBM per device.

```python
import jax
import jax.numpy as jnp
from jax import lax

D = 2560
HS = 256
FF = 7680
SEQS = 1
W = 2560
LENGTH = 1280


def draw_decay_param(key, part):
    values = jax.random.uniform(key, (W,), jnp.float32, -13.0, -5.0)
    return values


def raised(drawn, own_key, source, target, shards_of, factor):
    def block_of(axis_at):
        return (jnp.arange(drawn.shape[axis_at]) // (drawn.shape[axis_at] // shards_of)).reshape((-1,) + (1,) * (drawn.ndim - 1 - axis_at))

    first = jax.random.permutation(own_key, shards_of)[block_of(target)]
    second = (block_of(target) + shards_of // 2) % shards_of
    return jnp.where((block_of(source) == first) | (block_of(source) == second), factor * drawn, drawn)


def block_scale(key, shape, pieces, least, top_value):
    def one(dim, parts):
        draws = jax.random.uniform(jax.random.fold_in(jax.random.fold_in(key, 6), dim), (parts,), jnp.float32, least / len(pieces), top_value / len(pieces))
        return jnp.repeat(jnp.exp(draws), shape[dim] // parts).reshape((-1,) + (1,) * (len(shape) - dim - 1))

    loudness = one(*pieces[0])
    for cut in pieces[1:]:
        loudness = loudness * one(*cut)
    return loudness


def bell_draw(key, shape, width, reach, shards=(), held_as=jnp.bfloat16):
    gain = block_scale(key, shape, shards, -0.22, 0.18) if shards else 1.0
    drawn = jax.random.normal(key, shape, jnp.float32) * width * gain
    return jnp.minimum(jnp.maximum(drawn, -reach), reach).astype(held_as)


def noise_with(own_key, extent, deviation, most, pieces, heavy, held_as=jnp.bfloat16):
    array = deviation * jax.random.normal(own_key, extent, jnp.float32)
    if pieces:
        array = array * block_scale(own_key, extent, pieces, -0.22, 0.18)
    return jnp.clip(raised(array, jax.random.fold_in(own_key, 3), *heavy), -most, most).astype(held_as)


def setup_inputs(seed: int = 0) -> dict:
    keys = jax.random.split(jax.random.key(seed), 16)
    block_input = bell_draw(keys[0], (SEQS, LENGTH, D), 1.0, 6.0, ((1, 8),))
    mix_gain = jnp.clip(1.0 + 0.1 * jax.random.normal(keys[1], (D,), jnp.float32), 0.5, 1.5)
    x_weight = bell_draw(keys[2], (D, W), D ** -0.5, 0.125, ((1, 4),))
    y_weight = bell_draw(keys[3], (D, W), D ** -0.5, 0.125, ((1, 4),))
    conv_weight = bell_draw(keys[4], (4, W), 4 ** -0.5, 3.0, ((1, 4),), jnp.float32)
    conv_bias = bell_draw(keys[5], (W,), 0.5, 3.0, ((0, 4),), jnp.float32)
    input_gate = bell_draw(keys[6], (HS, W), HS ** -0.5, 0.375, ((1, 4),))
    decay_gate = bell_draw(keys[7], (HS, W), HS ** -0.5, 0.375, ((1, 4),))
    decay_param = draw_decay_param(jax.random.fold_in(keys[15], 71), 0)
    out_weight = bell_draw(keys[9], (W, D), W ** -0.5, 0.125, ((0, 4),))
    ffn_gain = jnp.clip(1.0 + 0.1 * jax.random.normal(keys[10], (D,), jnp.float32), 0.5, 1.5)
    gate_weight = bell_draw(keys[11], (D, FF), D ** -0.5, 0.125, ((1, 4),))
    up_weight = bell_draw(keys[12], (D, FF), D ** -0.5, 0.125, ((1, 4),))
    down_weight = bell_draw(keys[13], (FF, D), FF ** -0.5, 0.0625, ((0, 4),))
    out_cotangent = noise_with(keys[14], (SEQS, LENGTH, D), 1.0, 6.0, ((1, 8),), (1, 2, 8, 2.0))
    return {"block_input": block_input, "mix_gain": mix_gain, "x_weight": x_weight, "y_weight": y_weight, "conv_weight": conv_weight, "conv_bias": conv_bias, "input_gate": input_gate, "decay_gate": decay_gate, "decay_param": decay_param, "out_weight": out_weight, "ffn_gain": ffn_gain, "gate_weight": gate_weight, "up_weight": up_weight, "down_weight": down_weight, "out_cotangent": out_cotangent}


EPS = 1e-06

def gelu_tanh(values):
    return jax.nn.gelu(values, approximate=True)

def gelu_slope(values):
    _, pullback = jax.vjp(gelu_tanh, values)
    return pullback(jnp.ones_like(values))[0]

def bdot(left, right):
    return jnp.dot(left, right, preferred_element_type=jnp.float32)

def one_sequence(seq_input, seq_cot, mix_gain, x_weight, y_weight, conv_weight, conv_bias, input_gate, decay_gate, decay_param, out_weight, ffn_gain, gate_weight, up_weight, down_weight):
    length = seq_input.shape[0]
    chans = x_weight.shape[1]
    head_size = input_gate.shape[0]
    head_count = chans // head_size
    gate_mat_x = input_gate.astype(jnp.float32).reshape(head_size, head_count, head_size).transpose(1, 0, 2)
    gate_mat_a = decay_gate.astype(jnp.float32).reshape(head_size, head_count, head_size).transpose(1, 0, 2)
    inp = seq_input.astype(jnp.float32)
    r_one = lax.rsqrt(lax.optimization_barrier(jnp.mean(inp * inp, axis=-1, keepdims=True)) + EPS)
    n_one = inp * r_one
    normed1 = (n_one * mix_gain).astype(jnp.bfloat16)
    x_branch = bdot(normed1, x_weight)
    y_branch = bdot(normed1, y_weight)
    y_gated = gelu_tanh(y_branch)
    padded = jnp.concatenate([jnp.zeros((3, chans), jnp.float32), x_branch], axis=0)
    conv_out = conv_bias + sum((conv_weight[offset] * padded[offset:offset + length] for offset in range(4)))
    conv_low = conv_out.astype(jnp.bfloat16)
    heads = conv_low.astype(jnp.float32).reshape(length, head_count, head_size)
    gate_x = jax.nn.sigmoid(jnp.einsum('thi,hij->thj', heads, gate_mat_x).reshape(length, chans))
    gate_a = jax.nn.sigmoid(jnp.einsum('thi,hij->thj', heads, gate_mat_a).reshape(length, chans))
    softer = jax.nn.softplus(decay_param)
    log_decay = -8.0 * softer * gate_a
    decay = jnp.exp(log_decay)
    mult = jnp.sqrt(-jnp.expm1(2.0 * log_decay))
    drive = conv_out * gate_x * mult

    def forward_step(state, pair):
        state = pair[0] * state + pair[1]
        return (state, state)
    _, hidden = lax.scan(forward_step, jnp.zeros((chans,), jnp.float32), (decay, drive))
    mixed = (hidden * y_gated).astype(jnp.bfloat16)
    x_one = inp + bdot(mixed, out_weight)
    r_two = lax.rsqrt(lax.optimization_barrier(jnp.mean(x_one * x_one, axis=-1, keepdims=True)) + EPS)
    n_two = x_one * r_two
    normed2 = (n_two * ffn_gain).astype(jnp.bfloat16)
    gate_pre = bdot(normed2, gate_weight)
    up_pre = bdot(normed2, up_weight)
    act = (gelu_tanh(gate_pre) * up_pre).astype(jnp.bfloat16)
    output = (x_one + bdot(act, down_weight)).astype(jnp.bfloat16)
    cot = seq_cot.astype(jnp.float32)
    d_act = bdot(seq_cot, down_weight.T)
    g_down = bdot(act.T, seq_cot)
    d_gate = (d_act * up_pre * gelu_slope(gate_pre)).astype(jnp.bfloat16)
    d_up = (d_act * gelu_tanh(gate_pre)).astype(jnp.bfloat16)
    g_gate = bdot(normed2.T, d_gate)
    g_up = bdot(normed2.T, d_up)
    d_n_two = bdot(d_gate, gate_weight.T) + bdot(d_up, up_weight.T)
    g_ffn_gain = lax.optimization_barrier(jnp.sum(d_n_two * n_two, axis=0))
    e_two = ffn_gain * d_n_two
    d_x_one = cot + r_two * (e_two - n_two * lax.optimization_barrier(jnp.mean(e_two * n_two, axis=-1, keepdims=True)))
    d_x_low = d_x_one.astype(jnp.bfloat16)
    g_out = bdot(mixed.T, d_x_low)
    d_mixed = bdot(d_x_low, out_weight.T)
    d_y_low = (d_mixed * hidden * gelu_slope(y_branch)).astype(jnp.bfloat16)
    direct = d_mixed * y_gated
    decay_next = jnp.concatenate([decay[1:], jnp.zeros((1, chans), jnp.float32)], axis=0)

    def backward_step(carry, pair):
        value = pair[1] + pair[0] * carry
        return (value, value)
    _, lam = lax.scan(backward_step, jnp.zeros((chans,), jnp.float32), (decay_next, direct), reverse=True)
    hidden_prev = jnp.concatenate([jnp.zeros((1, chans), jnp.float32), hidden[:-1]], axis=0)
    d_log = lam * hidden_prev * decay - lam * conv_out * gate_x * decay * decay / mult
    g_decay = lax.optimization_barrier(jnp.sum(d_log * (-8.0 * gate_a) * jax.nn.sigmoid(decay_param), axis=0))
    d_gx = (lam * conv_out * mult * gate_x * (1.0 - gate_x)).astype(jnp.bfloat16)
    d_ga = (d_log * (-8.0 * softer) * gate_a * (1.0 - gate_a)).astype(jnp.bfloat16)
    d_gx_heads = d_gx.astype(jnp.float32).reshape(length, head_count, head_size)
    d_ga_heads = d_ga.astype(jnp.float32).reshape(length, head_count, head_size)
    g_input_gate = jnp.einsum('thi,thj->hij', heads, d_gx_heads).transpose(1, 0, 2).reshape(head_size, chans)
    g_decay_gate = jnp.einsum('thi,thj->hij', heads, d_ga_heads).transpose(1, 0, 2).reshape(head_size, chans)
    back_x = jnp.einsum('thj,hij->thi', d_gx_heads, gate_mat_x).reshape(length, chans)
    back_a = jnp.einsum('thj,hij->thi', d_ga_heads, gate_mat_a).reshape(length, chans)
    d_conv = lam * gate_x * mult + back_x + back_a
    g_conv_bias = lax.optimization_barrier(jnp.sum(d_conv, axis=0))
    g_conv = jnp.stack([lax.optimization_barrier(jnp.sum(d_conv * padded[offset:offset + length], axis=0)) for offset in range(4)])
    padded_back = jnp.concatenate([d_conv, jnp.zeros((3, chans), jnp.float32)], axis=0)
    d_x_branch = sum((conv_weight[offset] * padded_back[3 - offset:3 - offset + length] for offset in range(4)))
    d_x_branch = d_x_branch.astype(jnp.bfloat16)
    g_x = bdot(normed1.T, d_x_branch)
    g_y = bdot(normed1.T, d_y_low)
    d_n_one = bdot(d_x_branch, x_weight.T) + bdot(d_y_low, y_weight.T)
    g_mix_gain = lax.optimization_barrier(jnp.sum(d_n_one * n_one, axis=0))
    e_one = mix_gain * d_n_one
    d_input = (d_x_one + r_one * (e_one - n_one * lax.optimization_barrier(jnp.mean(e_one * n_one, axis=-1, keepdims=True)))).astype(jnp.bfloat16)
    grads = (g_mix_gain, g_x, g_y, g_conv, g_conv_bias, g_input_gate, g_decay_gate, g_decay, g_out, g_ffn_gain, g_gate, g_up, g_down)
    return (output, d_input, grads)

def reference(block_input, mix_gain, x_weight, y_weight, conv_weight, conv_bias, input_gate, decay_gate, decay_param, out_weight, ffn_gain, gate_weight, up_weight, down_weight, out_cotangent):
    weights = (mix_gain, x_weight, y_weight, conv_weight, conv_bias, input_gate, decay_gate, decay_param, out_weight, ffn_gain, gate_weight, up_weight, down_weight)
    zero_grads = tuple((jnp.zeros(item.shape, jnp.float32) for item in weights))

    def per_sequence(totals, pair):
        output, d_input, grads = one_sequence(pair[0], pair[1], *weights)
        totals = tuple((total + grad for total, grad in zip(totals, grads)))
        return (totals, (output, d_input))
    totals, (outputs, d_inputs) = lax.scan(per_sequence, zero_grads, (block_input, out_cotangent))
    return (outputs, d_inputs, totals[0], totals[1], totals[2], totals[3], totals[4], totals[5], totals[6], totals[7], totals[8], totals[9], totals[10], totals[11], totals[12])
```

```python
import functools

import jax
import jax.numpy as jnp
from jax import lax
from jax.experimental import pallas as pl
from jax.experimental.pallas import tpu as pltpu
from jax.sharding import PartitionSpec as P

EPS = 1e-06
GELU_K = 0.7978845608028654
GELU_C = 0.044715


def bdot(left, right):
    return jnp.dot(left, right, preferred_element_type=jnp.float32)


def tdot(left, right):
    return lax.dot_general(
        left, right, (((0,), (0,)), ((), ())), preferred_element_type=jnp.float32
    )


def dot_t(left, right):
    return lax.dot_general(
        left, right, (((1,), (1,)), ((), ())), preferred_element_type=jnp.float32
    )


def gelu_parts(values):
    t = jnp.tanh(GELU_K * (values + GELU_C * values * values * values))
    half = 0.5 * (1.0 + t)
    gelu = values * half
    slope = half + 0.5 * values * (1.0 - t * t) * GELU_K * (1.0 + 3.0 * GELU_C * values * values)
    return gelu, slope


def swap(value, axis, bit):
    size = lax.axis_size(axis)
    return lax.ppermute(value, axis, [(i, i ^ bit) for i in range(size)])


def shifted(value, axis, by):
    size = lax.axis_size(axis)
    return lax.ppermute(value, axis, [(i, i + by) for i in range(size) if 0 <= i + by < size])


def turned(value, axis, by):
    size = lax.axis_size(axis)
    return lax.ppermute(value, axis, [(i, (i + by) % size) for i in range(size)])


def scan_kernel(reverse, a_ref, u_ref, p_ref, h_ref):
    rows, width = a_ref.shape
    groups = rows // 8
    row = lax.broadcasted_iota(jnp.int32, (8, width), 0)
    carry_p = jnp.ones((8, width), jnp.float32)
    carry_h = jnp.zeros((8, width), jnp.float32)
    for step in range(groups):
        at = (groups - 1 - step if reverse else step) * 8
        a = a_ref[at : at + 8, :]
        u = u_ref[at : at + 8, :]
        for k in (1, 2, 4):
            shift = 8 - k if reverse else k
            valid = row < 8 - k if reverse else row >= k
            a_far = jnp.where(valid, pltpu.roll(a, shift, 0), 1.0)
            u_far = jnp.where(valid, pltpu.roll(u, shift, 0), 0.0)
            u = u + a * u_far
            a = a * a_far
        p = a * carry_p
        h = u + a * carry_h
        p_ref[at : at + 8, :] = p
        h_ref[at : at + 8, :] = h
        end = 0 if reverse else 7
        carry_p = jnp.broadcast_to(p[end : end + 1, :], (8, width))
        carry_h = jnp.broadcast_to(h[end : end + 1, :], (8, width))


def local_scan(decay, drive, reverse):
    shape = jax.ShapeDtypeStruct(decay.shape, jnp.float32)
    count = decay.shape[0] * decay.shape[1]
    return pl.pallas_call(
        functools.partial(scan_kernel, reverse),
        out_shape=(shape, shape),
        cost_estimate=pl.CostEstimate(
            flops=20 * count, bytes_accessed=16 * count, transcendentals=0
        ),
        name="scan_back" if reverse else "scan_fwd",
    )(decay, drive)


def carried(prod, end, reverse):
    size = lax.axis_size("seq")
    mine = lax.axis_index("seq")
    total = jnp.stack([prod, end])
    before = jnp.stack([jnp.ones_like(prod), jnp.zeros_like(end)])

    def join(first, second):
        return jnp.stack([first[0] * second[0], second[0] * first[1] + second[1]])

    bit = 1
    while bit < size:
        other = swap(total, "seq", bit)
        other_first = ((mine // bit) % 2 == 1) != reverse
        before = jnp.where(other_first, join(other, before), before)
        total = jnp.where(other_first, join(other, total), join(total, other))
        bit *= 2
    return before[1]


def pair_sum(keep, send):
    total = keep + swap(send, "mp", 1)
    bit = 2
    while bit < lax.axis_size("mp"):
        low = total.astype(jnp.bfloat16)
        total = low.astype(jnp.float32) + swap(low, "mp", bit).astype(jnp.float32)
        bit *= 2
    return total


def per_device(
    block_input,
    mix_gain,
    x_weight,
    y_weight,
    conv_weight,
    conv_bias,
    input_gate,
    decay_gate,
    decay_param,
    out_weight,
    ffn_gain,
    gate_weight,
    up_weight,
    down_weight,
    out_cotangent,
):
    seq_count, group_len, width = block_input.shape
    local_w = x_weight.shape[1]
    head = input_gate.shape[0]
    rest = local_w % head
    blocks = lax.axis_size("seq")
    place = lax.axis_index("seq")
    owner = lax.axis_index("mp")
    odd = owner % 2
    rows = group_len
    half = rows // 2
    cols = width // blocks

    def own(value):
        return lax.dynamic_slice_in_dim(value, odd * half, half, 0)

    def partner(value):
        return lax.dynamic_slice_in_dim(value, (1 - odd) * half, half, 0)

    def in_order(mine, other):
        first = jnp.where(odd == 1, other, mine)
        second = jnp.where(odd == 1, mine, other)
        return jnp.concatenate([first, second], axis=0)

    x_low = block_input.reshape(rows, width)
    cot_low = out_cotangent.reshape(rows, width)

    cot_own = own(cot_low)
    cot_rolled = jnp.concatenate([cot_own, partner(cot_low)], axis=0)
    cot_mine = lax.all_gather(cot_own, "seq", axis=0, tiled=True)
    cot_all = jnp.concatenate([cot_mine, swap(cot_mine, "mp", 1)], axis=0)

    inp_tail = shifted(x_low[rows - 8 :], "seq", 1)

    def norm_one(low):
        value = low.astype(jnp.float32)
        r = lax.rsqrt(jnp.mean(value * value, axis=-1, keepdims=True) + EPS)
        return r, value * r

    r_one, n_one = norm_one(x_low)
    normed1 = (n_one * mix_gain).astype(jnp.bfloat16)
    _, n_tail = norm_one(inp_tail)
    tail_low = (n_tail * mix_gain).astype(jnp.bfloat16)
    x_branch = bdot(normed1, x_weight)
    x_tail = bdot(tail_low, x_weight)
    y_branch = bdot(normed1, y_weight)
    padded = jnp.concatenate([x_tail[5:], x_branch], axis=0)
    conv_out = conv_bias + sum(
        conv_weight[offset] * padded[offset : offset + rows] for offset in range(4)
    )
    conv_low = conv_out.astype(jnp.bfloat16)

    far = swap(
        jnp.where(odd == 1, conv_low[:, :rest], conv_low[:, local_w - rest :]), "mp", 1
    )
    ext = jnp.concatenate([far, conv_low, far], axis=1)
    ext_w = local_w + 2 * rest
    start = owner * local_w - rest
    shift = start % head
    copies = -(-(ext_w + head - 1) // head)
    row_heads = (start + jnp.arange(ext_w, dtype=jnp.int32) + head) // head
    col_heads = (owner * local_w + jnp.arange(local_w, dtype=jnp.int32) + head) // head
    mask = row_heads[:, None] == col_heads[None, :]

    def dense(gate):
        tall = lax.dynamic_slice_in_dim(jnp.tile(gate, (copies, 1)), shift, ext_w, 0)
        return jnp.where(mask, tall, jnp.zeros((), gate.dtype))

    dense_both = jnp.concatenate([dense(input_gate), dense(decay_gate)], axis=1)
    gates = jax.nn.sigmoid(bdot(ext, dense_both))
    gate_x = gates[:, :local_w]
    gate_a = gates[:, local_w:]
    softer = jax.nn.softplus(decay_param)
    log_decay = -8.0 * softer * gate_a
    decay = jnp.exp(log_decay)
    mult = jnp.sqrt(-jnp.expm1(2.0 * log_decay))
    drive = conv_out * gate_x * mult
    prod, local_state = local_scan(decay, drive, False)
    block_prod = prod[rows - 1]
    state_in = carried(block_prod, local_state[rows - 1], False)
    hidden = local_state + prod * state_in
    y_gated, y_slope = gelu_parts(y_branch)
    mixed = (hidden * y_gated).astype(jnp.bfloat16)

    total_one = pair_sum(bdot(own(mixed), out_weight), bdot(partner(mixed), out_weight))
    mixed_all = lax.all_gather(mixed, "seq", axis=0, tiled=True)
    x_one = own(x_low).astype(jnp.float32) + total_one
    r_two = lax.rsqrt(jnp.mean(x_one * x_one, axis=-1, keepdims=True) + EPS)
    n_two = x_one * r_two
    normed2_own = (n_two * ffn_gain).astype(jnp.bfloat16)
    normed2 = jnp.concatenate([normed2_own, swap(normed2_own, "mp", 1)], axis=0)
    normed2_mine = lax.all_gather(normed2_own, "seq", axis=0, tiled=True)
    normed2_all = jnp.concatenate([normed2_mine, swap(normed2_mine, "mp", 1)], axis=0)

    def ffn(normed, cot):
        gate_gelu, gate_slope = gelu_parts(bdot(normed, gate_weight))
        up_pre = bdot(normed, up_weight)
        d_act = dot_t(cot, down_weight)
        act = (gate_gelu * up_pre).astype(jnp.bfloat16)
        d_gate = (d_act * up_pre * gate_slope).astype(jnp.bfloat16)
        d_up = (d_act * gate_gelu).astype(jnp.bfloat16)
        return act, d_gate, d_up

    act, d_gate, d_up = ffn(normed2, cot_rolled)
    part_two = [
        dot_t(d_gate[at : at + half], gate_weight) + dot_t(d_up[at : at + half], up_weight)
        for at in (half, 0)
    ]
    d_n_two = pair_sum(part_two[1], part_two[0])
    part_out = bdot(act, down_weight)
    ffn_out = pair_sum(part_out[:half], part_out[half:])
    out_own = (x_one + ffn_out).astype(jnp.bfloat16)
    block_output = in_order(out_own, swap(out_own, "mp", 1))

    g_ffn_gain = jnp.sum(d_n_two * n_two, axis=0)
    e_two = ffn_gain * d_n_two
    d_x_one = cot_own.astype(jnp.float32) + r_two * (
        e_two - n_two * jnp.mean(e_two * n_two, axis=-1, keepdims=True)
    )
    d_x_low_own = d_x_one.astype(jnp.bfloat16)
    d_x_low = in_order(d_x_low_own, swap(d_x_low_own, "mp", 1))

    d_mixed = dot_t(d_x_low, out_weight)
    d_y_low = (d_mixed * hidden * y_slope).astype(jnp.bfloat16)
    decay_next = jnp.concatenate([decay[1:], jnp.ones((1, local_w), jnp.float32)], axis=0)
    after_prod, local_lam = local_scan(decay_next, d_mixed * y_gated, True)
    returned = carried(block_prod, decay[0] * local_lam[0], True)
    lam = local_lam + after_prod * returned
    hidden_prev = jnp.concatenate([state_in[None, :], hidden[:-1]], axis=0)
    d_log = lam * hidden_prev * decay - lam * conv_out * gate_x * decay * decay / mult
    g_decay = jnp.sum(d_log * (-8.0 * gate_a) * jax.nn.sigmoid(decay_param), axis=0)
    d_gx = (lam * conv_out * mult * gate_x * (1.0 - gate_x)).astype(jnp.bfloat16)
    d_ga = (d_log * (-8.0 * softer) * gate_a * (1.0 - gate_a)).astype(jnp.bfloat16)
    d_both = jnp.concatenate([d_gx, d_ga], axis=1)
    back = dot_t(d_both, dense_both)
    far_back = swap(
        jnp.where(odd == 1, back[:, :rest], back[:, ext_w - rest :]), "mp", 1
    )
    zeros = jnp.zeros((rows, local_w - rest), jnp.float32)
    back_own = back[:, rest : rest + local_w] + jnp.where(
        odd == 1,
        jnp.concatenate([far_back, zeros], axis=1),
        jnp.concatenate([zeros, far_back], axis=1),
    )
    d_conv = lam * gate_x * mult + back_own
    g_conv_bias = jnp.sum(d_conv, axis=0)
    g_conv = jnp.stack(
        [jnp.sum(d_conv * padded[offset : offset + rows], axis=0) for offset in range(4)]
    )
    later = shifted(d_conv[:8], "seq", -1)
    padded_back = jnp.concatenate([d_conv, later[:3]], axis=0)
    d_x_branch = sum(
        conv_weight[offset] * padded_back[3 - offset : 3 - offset + rows] for offset in range(4)
    ).astype(jnp.bfloat16)
    d_branches = lax.all_gather(
        jnp.concatenate([d_y_low, d_x_branch], axis=1), "seq", axis=0, tiled=True
    )

    def d_n_part(pick):
        return dot_t(pick(d_x_branch), x_weight) + dot_t(pick(d_y_low), y_weight)

    d_n_send = d_n_part(partner)
    d_n_keep = d_n_part(own)
    d_n_one = pair_sum(d_n_keep, d_n_send)
    n_one_own = own(n_one)
    g_mix_gain = jnp.sum(d_n_one * n_one_own, axis=0)
    e_one = mix_gain * d_n_one
    d_input = d_x_one + own(r_one) * (
        e_one - n_one_own * jnp.mean(e_one * n_one_own, axis=-1, keepdims=True)
    )
    in_own = d_input.astype(jnp.bfloat16)
    input_grad = in_order(in_own, swap(in_own, "mp", 1))

    d_dense = tdot(ext, d_both)
    d_dense = jnp.where(jnp.concatenate([mask, mask], axis=1), d_dense, 0.0)
    tall = lax.dynamic_update_slice_in_dim(
        jnp.zeros((copies * head, 2 * local_w), jnp.float32), d_dense, shift, 0
    )
    g_gates = jnp.sum(tall.reshape(copies, head, 2 * local_w), axis=0)
    g_gates = g_gates.reshape(blocks, head // blocks, 2 * local_w)
    vectors = jnp.concatenate([g_conv, g_conv_bias[None], g_decay[None]], axis=0)
    vectors = vectors.reshape(6, blocks, local_w // blocks).transpose(1, 0, 2)
    gains = jnp.stack([g_ffn_gain, g_mix_gain]).reshape(2, blocks, cols).transpose(1, 0, 2)
    g_gates = lax.psum_scatter(g_gates, "seq", scatter_dimension=0, tiled=True)[0]
    vectors = lax.psum_scatter(vectors, "seq", scatter_dimension=0, tiled=True)[0]
    gains = lax.psum_scatter(gains, "seq", scatter_dimension=0, tiled=True)[0]
    gains = gains + swap(gains, "mp", 1)

    both = jnp.stack([own(normed1), d_x_low_own])
    both = both.reshape(2, half, blocks, cols).transpose(2, 0, 1, 3)
    both = lax.all_to_all(both, "seq", split_axis=0, concat_axis=0, tiled=True)
    far_both = swap(both, "mp", 1)
    first = jnp.where(odd == 1, far_both, both)
    second = jnp.where(odd == 1, both, far_both)
    both = jnp.stack([first, second], axis=2)
    normed1_cols = both[:, 0].reshape(blocks * rows, cols)
    d_x_cols = both[:, 1].reshape(blocks * rows, cols)
    g_out = tdot(mixed_all, d_x_cols)
    g_y = tdot(normed1_cols, d_branches[:, :local_w])
    g_x = tdot(normed1_cols, d_branches[:, local_w:])

    act_all, d_gate_all, d_up_all = ffn(normed2_all, cot_all)
    normed2_cols = lax.dynamic_slice_in_dim(normed2_all, place * cols, cols, 1)
    cot_cols = lax.dynamic_slice_in_dim(cot_all, place * cols, cols, 1)
    g_gate = tdot(normed2_cols, d_gate_all)
    g_up = tdot(normed2_cols, d_up_all)
    g_down = tdot(act_all, cot_cols)

    shape = (seq_count, group_len, width)
    return (
        block_output.reshape(shape),
        input_grad.reshape(shape),
        gains[1],
        g_x,
        g_y,
        vectors[:4],
        vectors[4],
        g_gates[:, :local_w],
        g_gates[:, local_w:],
        vectors[5],
        g_out,
        gains[0],
        g_gate,
        g_up,
        g_down,
    )


def solution(mesh):
    in_specs = (
        P(None, "seq", None),
        P(),
        P(None, "mp"),
        P(None, "mp"),
        P(None, "mp"),
        P("mp"),
        P(None, "mp"),
        P(None, "mp"),
        P("mp"),
        P("mp", None),
        P(),
        P(None, "mp"),
        P(None, "mp"),
        P("mp", None),
        P(None, "seq", None),
    )
    out_specs = (
        P(None, "seq", None),
        P(None, "seq", None),
        P("seq"),
        P("seq", "mp"),
        P("seq", "mp"),
        P(None, ("mp", "seq")),
        P(("mp", "seq")),
        P("seq", "mp"),
        P("seq", "mp"),
        P(("mp", "seq")),
        P("mp", "seq"),
        P("seq"),
        P("seq", "mp"),
        P("seq", "mp"),
        P("mp", "seq"),
    )
    return jax.shard_map(
        per_device, mesh=mesh, in_specs=in_specs, out_specs=out_specs, check_vma=False
    )
```

```python
import functools

import jax
import jax.numpy as jnp
from jax import lax
from jax.experimental import pallas as pl
from jax.experimental.pallas import tpu as pltpu
from jax.sharding import PartitionSpec as P


EPS = 1e-06
GELU_K = 0.7978845608028654
GELU_C = 0.044715
MIB = 1024 * 1024
SMALL_VMEM = 32 * MIB


def bdot(left, right):
    return jnp.dot(left, right, preferred_element_type=jnp.float32)


def tdot(left, right):
    return lax.dot_general(
        left, right, (((0,), (0,)), ((), ())), preferred_element_type=jnp.float32
    )


def dot_t(left, right):
    return lax.dot_general(
        left, right, (((1,), (1,)), ((), ())), preferred_element_type=jnp.float32
    )


def gelu_parts(values):
    square = values * values
    t = jnp.tanh(values * (GELU_K + (GELU_K * GELU_C) * square))
    half = 0.5 + 0.5 * t
    bend = values * (0.5 * GELU_K + (1.5 * GELU_K * GELU_C) * square)
    return values * half, half + bend * (1.0 - t * t)


def swap(value, axis, bit):
    size = lax.axis_size(axis)
    return lax.ppermute(value, axis, [(i, i ^ bit) for i in range(size)])


def shifted(value, axis, by):
    size = lax.axis_size(axis)
    return lax.ppermute(value, axis, [(i, i + by) for i in range(size) if 0 <= i + by < size])


def scan_rows(reverse, a_at, u_at, rows, store):
    groups = rows // 8
    carry_p = carry_h = None
    for step in range(groups):
        at = (groups - 1 - step if reverse else step) * 8
        a = a_at(at)
        u = u_at(at)
        row = lax.broadcasted_iota(jnp.int32, a.shape, 0)
        for k in (1, 2, 4):
            shift = 8 - k if reverse else k
            valid = row < 8 - k if reverse else row >= k
            a_far = jnp.where(valid, pltpu.roll(a, shift, 0), 1.0)
            u_far = jnp.where(valid, pltpu.roll(u, shift, 0), 0.0)
            u = u + a * u_far
            a = a * a_far
        if carry_p is not None:
            u = u + a * carry_h
            a = a * carry_p
        store(at, a, u)
        end = 0 if reverse else 7
        carry_p = jnp.broadcast_to(a[end : end + 1, :], a.shape)
        carry_h = jnp.broadcast_to(u[end : end + 1, :], a.shape)
    return carry_p[0:1], carry_h[0:1]


def head_blocks(odd, local_w, head):
    rest = local_w % head
    full = local_w // head
    if odd:
        blocks = [(0, rest, [(0, rest, "far", 0, rest), (rest, head, "own", 0, rest)])]
        first = rest
    else:
        at = full * head
        blocks = [
            (at, local_w, [(0, rest, "own", at, local_w), (rest, head, "far", 0, rest)])
        ]
        first = 0
    for j in range(full):
        lo = first + j * head
        blocks.append((lo, lo + head, [(0, head, "own", lo, lo + head)]))
    return blocks


def either(odd_ref, body):
    odd = odd_ref[0]

    @pl.when(odd == 0)
    def _():
        body(0)

    @pl.when(odd == 1)
    def _():
        body(1)


def norm_rows(low):
    value = low.astype(jnp.float32)
    r = lax.rsqrt(jnp.mean(value * value, axis=-1, keepdims=True) + EPS)
    return r, value * r


def softplus(value):
    e = jnp.exp(-jnp.abs(value))
    series = 1.0 / 9.0
    for k in (8.0, 7.0, 6.0, 5.0, 4.0, 3.0, 2.0, 1.0):
        series = 1.0 / k - e * series
    return jnp.maximum(value, 0.0) + jnp.where(e < 0.125, e * series, jnp.log(1.0 + e))


def in_hbm(*values):
    return [pltpu.with_memory_space_constraint(v, pltpu.HBM) for v in values]


def kept(shape, dtype):
    return pltpu.HBM(shape, dtype)


def begin(*copies):
    for copy in copies:
        copy.start()
    return copies


def front_kernel(
    odd_ref, tail_ref, x_hbm, gain_hbm, xw_hbm, yw_hbm, cw_hbm, cb_hbm, decay_hbm,
    conv_ref, low_ref, gated_ref, far_ref, soft_ref,
    normed_hbm, r_hbm, pad_hbm, slope_hbm, sig_hbm, conv_hbm, low_hbm, gated_hbm, soft_hbm,
    held, y_s, x_s, gain_s, xw_s, yw_s, cw_s, cb_s, decay_s, r_ref, pad_ref, slope_ref, sig_ref,
    sems, out_sems,
):
    rows = x_s.shape[0]
    steps, tk, local_w = xw_s.shape
    rest = far_ref.shape[1]
    copy = pltpu.make_async_copy
    x_copy, gain_copy = begin(
        copy(x_hbm, x_s, sems.at[0]), copy(gain_hbm, gain_s, sems.at[1])
    )
    weights = [
        begin(
            copy(xw_hbm.at[k * tk : (k + 1) * tk, :], xw_s.at[k], sems.at[5 + 2 * k]),
            copy(yw_hbm.at[k * tk : (k + 1) * tk, :], yw_s.at[k], sems.at[6 + 2 * k]),
        )
        for k in range(steps)
    ]
    last = begin(
        copy(cw_hbm, cw_s, sems.at[2]),
        copy(cb_hbm, cb_s, sems.at[3]),
        copy(decay_hbm, decay_s, sems.at[4]),
    )
    x_copy.wait()
    gain_copy.wait()
    gain = gain_s[...].reshape(1, gain_s.shape[0])
    r, n = norm_rows(x_s[...])
    r_ref[...] = r
    held[0:rows, :] = (n * gain).astype(jnp.bfloat16)
    outs = list(
        begin(
            copy(held.at[0:rows, :], normed_hbm, out_sems.at[0]),
            copy(r_ref, r_hbm, out_sems.at[1]),
        )
    )
    _, n = norm_rows(tail_ref[...])
    held[rows : rows + 8, :] = (n * gain).astype(jnp.bfloat16)
    pad_ref[...] = jnp.zeros_like(pad_ref)
    y_s[...] = jnp.zeros_like(y_s)
    for k, pair in enumerate(weights):
        at = slice(k * tk, (k + 1) * tk)
        for part in pair:
            part.wait()
        both = bdot(held[:, at], xw_s[k])
        pad_ref[0:8, :] += both[rows : rows + 8]
        pad_ref[8 : rows + 8, :] += both[0:rows]
        y_s[...] += bdot(held[0:rows, at], yw_s[k])
    outs += begin(copy(pad_ref, pad_hbm, out_sems.at[2]))
    for part in last:
        part.wait()
    param = decay_s[...].reshape(1, local_w)
    soft_ref[...] = softplus(param)
    sig_ref[...] = jax.nn.sigmoid(param)
    conv = cb_s[...].reshape(1, local_w) + cw_s[3:4, :] * pad_ref[8 : rows + 8, :]
    for offset in range(3):
        taps = pad_ref[5 + offset : 5 + offset + rows, :]
        conv = conv + cw_s[offset : offset + 1, :] * taps
    conv_ref[...] = conv
    low = conv.astype(jnp.bfloat16)
    low_ref[...] = low
    outs += begin(
        copy(conv_ref, conv_hbm, out_sems.at[3]),
        copy(low_ref, low_hbm, out_sems.at[4]),
        copy(sig_ref, sig_hbm, out_sems.at[5]),
        copy(soft_ref, soft_hbm, out_sems.at[6]),
    )

    def body(odd):
        lo = 0 if odd else local_w - rest
        far_ref[...] = low[:, lo : lo + rest]

    either(odd_ref, body)
    gelu, slope = gelu_parts(y_s[...])
    gated_ref[...] = gelu
    slope_ref[...] = slope
    outs += begin(
        copy(gated_ref, gated_hbm, out_sems.at[7]), copy(slope_ref, slope_hbm, out_sems.at[8])
    )
    for part in outs:
        part.wait()


def front(odd, x_low, tail, gain, xw, yw, cw, cb, decay_param, rest):
    rows, width = x_low.shape
    local_w = xw.shape[1]
    tk = 512
    steps = width // tk
    f32, bf16 = jnp.float32, jnp.bfloat16
    wide = jax.ShapeDtypeStruct((rows, local_w), f32)
    vmem = pl.BlockSpec(memory_space=pltpu.VMEM)
    hbm = pl.BlockSpec(memory_space=pltpu.HBM)
    line = jax.ShapeDtypeStruct((1, local_w), f32)
    return pl.pallas_call(
        front_kernel,
        in_specs=[pl.BlockSpec(memory_space=pltpu.SMEM), vmem] + [hbm] * 7,
        out_specs=[vmem] * 5 + [hbm] * 9,
        out_shape=(
            wide,
            jax.ShapeDtypeStruct((rows, local_w), bf16),
            wide,
            jax.ShapeDtypeStruct((rows, rest), bf16),
            line,
            kept((rows, width), bf16),
            kept((rows, 1), f32),
            kept((rows + 8, local_w), f32),
            kept((rows, local_w), f32),
            kept((1, local_w), f32),
            kept((rows, local_w), f32),
            kept((rows, local_w), bf16),
            kept((rows, local_w), f32),
            kept((1, local_w), f32),
        ),
        scratch_shapes=[
            pltpu.VMEM((rows + 8, width), bf16),
            pltpu.VMEM((rows, local_w), f32),
            pltpu.VMEM((rows, width), bf16),
            pltpu.VMEM((width,), f32),
            pltpu.VMEM((steps, tk, local_w), bf16),
            pltpu.VMEM((steps, tk, local_w), bf16),
            pltpu.VMEM((4, local_w), f32),
            pltpu.VMEM((local_w,), f32),
            pltpu.VMEM((local_w,), f32),
            pltpu.VMEM((rows, 1), f32),
            pltpu.VMEM((rows + 8, local_w), f32),
            pltpu.VMEM((rows, local_w), f32),
            pltpu.VMEM((1, local_w), f32),
            pltpu.SemaphoreType.DMA((5 + 2 * steps,)),
            pltpu.SemaphoreType.DMA((9,)),
        ],
        cost_estimate=pl.CostEstimate(
            flops=4 * rows * width * local_w,
            bytes_accessed=4 * width * local_w + 4 * rows * width,
            transcendentals=rows * local_w,
        ),
        compiler_params=pltpu.CompilerParams(vmem_limit_bytes=SMALL_VMEM),
        name="front",
    )(odd, tail, *in_hbm(x_low, gain, xw, yw, cw, cb, decay_param))


def small_call(kernel, outs, smem, *args):
    vmem = pl.BlockSpec(memory_space=pltpu.VMEM)
    scalars = [pl.BlockSpec(memory_space=pltpu.SMEM)] * len(smem)
    size = sum(a.size for a in args)
    return pl.pallas_call(
        kernel,
        in_specs=scalars + [vmem] * len(args),
        out_specs=[vmem] * len(outs),
        out_shape=tuple(jax.ShapeDtypeStruct(shape, dtype) for shape, dtype in outs),
        cost_estimate=pl.CostEstimate(flops=8 * size, bytes_accessed=8 * size, transcendentals=0),
        compiler_params=pltpu.CompilerParams(vmem_limit_bytes=SMALL_VMEM // 2),
    )(*smem, *args)


def half_call(kernel, odd, whole_rows, args, outs, held=()):
    spec = lambda a: pl.BlockSpec(a.shape, lambda i, odd_ref: (0,) * a.ndim)
    cut_spec = lambda a: pl.BlockSpec(
        (a.shape[0] // 2, a.shape[1]), lambda i, odd_ref: (odd_ref[0], 0)
    )
    size = sum(a.size for a in args)
    return pl.pallas_call(
        kernel,
        grid_spec=pltpu.PrefetchScalarGridSpec(
            num_scalar_prefetch=1,
            grid=(1,),
            in_specs=[cut_spec(a) for a in whole_rows] + [spec(a) for a in (*args, *held)],
            out_specs=[spec(jax.ShapeDtypeStruct(*o)) for o in outs],
        ),
        out_shape=tuple(kept(shape, dtype) for shape, dtype in outs),
        cost_estimate=pl.CostEstimate(flops=8 * size, bytes_accessed=8 * size, transcendentals=0),
        compiler_params=pltpu.CompilerParams(vmem_limit_bytes=SMALL_VMEM // 2),
    )(odd, *in_hbm(*whole_rows), *args, *in_hbm(*held))


def one_less_square(log_a, a):
    y = 2.0 * log_a
    series = 1.0 + y * (1.0 / 7.0)
    for k in (6.0, 5.0, 4.0, 3.0, 2.0):
        series = 1.0 + y * (1.0 / k) * series
    return jnp.where(y > -0.25, -y * series, 1.0 - a * a)


def gates_kernel(
    odd_ref, conv_ref, low_ref, far_ref, wx_ref, wa_ref, soft_ref,
    prod_ref, state_ref, total_ref, gx_hbm, ga_hbm, decay_hbm, mult_hbm, far_hbm, total_hbm,
    gx_ref, ga_ref, decay_ref, mult_ref, sems,
):
    rows, local_w = conv_ref.shape
    copy = pltpu.make_async_copy
    outs = list(begin(copy(far_ref, far_hbm, sems.at[0])))
    head = wx_ref.shape[0]

    def body(odd):
        src = {"own": low_ref, "far": far_ref}
        for lo, hi, parts in head_blocks(odd, local_w, head):
            for w_ref, g_ref in ((wx_ref, gx_ref), (wa_ref, ga_ref)):
                acc = None
                for r0, r1, name, s0, s1 in parts:
                    term = bdot(src[name][:, s0:s1], w_ref[r0:r1, lo:hi])
                    acc = term if acc is None else acc + term
                g_ref[:, lo:hi] = jax.nn.sigmoid(acc)

    either(odd_ref, body)
    outs += begin(copy(gx_ref, gx_hbm, sems.at[1]), copy(ga_ref, ga_hbm, sems.at[2]))
    log_decay = -8.0 * soft_ref[...] * ga_ref[...]
    decay = jnp.exp(log_decay)
    mult = jnp.sqrt(one_less_square(log_decay, decay))
    decay_ref[...] = decay
    mult_ref[...] = mult
    outs += begin(copy(decay_ref, decay_hbm, sems.at[3]), copy(mult_ref, mult_hbm, sems.at[4]))
    state_ref[...] = conv_ref[...] * gx_ref[...] * mult

    def store(at, p, h):
        prod_ref[at : at + 8, :] = p
        state_ref[at : at + 8, :] = h

    prod, end = scan_rows(
        False, lambda at: decay_ref[at : at + 8, :], lambda at: state_ref[at : at + 8, :], rows, store
    )
    total_ref[0:1, :] = prod
    total_ref[1:2, :] = end
    outs += begin(copy(total_ref, total_hbm, sems.at[5]))
    for part in outs:
        part.wait()


def gates(odd, conv, low, far, wx, wa, soft):
    rows, local_w = conv.shape
    head = wx.shape[0]
    f32 = jnp.float32
    wide = jax.ShapeDtypeStruct((rows, local_w), f32)
    vmem = pl.BlockSpec(memory_space=pltpu.VMEM)
    hbm = pl.BlockSpec(memory_space=pltpu.HBM)
    return pl.pallas_call(
        gates_kernel,
        in_specs=[pl.BlockSpec(memory_space=pltpu.SMEM)] + [vmem] * 6,
        out_specs=[vmem] * 3 + [hbm] * 6,
        out_shape=(wide, wide, jax.ShapeDtypeStruct((2, local_w), f32))
        + (kept((rows, local_w), f32),) * 4
        + (kept(far.shape, far.dtype), kept((2, local_w), f32)),
        scratch_shapes=[pltpu.VMEM((rows, local_w), f32)] * 4 + [pltpu.SemaphoreType.DMA((6,))],
        cost_estimate=pl.CostEstimate(
            flops=4 * rows * head * local_w + 60 * rows * local_w,
            bytes_accessed=40 * rows * local_w,
            transcendentals=6 * rows * local_w,
        ),
        compiler_params=pltpu.CompilerParams(vmem_limit_bytes=SMALL_VMEM),
        name="gates",
    )(odd, conv, low, far, wx, wa, soft)


def mix_kernel(
    odd_ref, state_in_ref, prod_ref, state_ref, gated_ref, w_hbm,
    mixed_ref, keep_ref, send_ref, hidden_hbm, state_in_hbm, w_s, sems, hidden_ref, out_sems,
):
    steps, _, tn = w_s.shape
    half = keep_ref.shape[0]
    copies = begin(
        *[
            pltpu.make_async_copy(w_hbm.at[:, j * tn : (j + 1) * tn], w_s.at[j], sems.at[j])
            for j in range(steps)
        ]
    )
    hidden = state_ref[...] + prod_ref[...] * state_in_ref[...]
    hidden_ref[...] = hidden
    outs = begin(
        pltpu.make_async_copy(hidden_ref, hidden_hbm, out_sems.at[0]),
        pltpu.make_async_copy(state_in_ref, state_in_hbm, out_sems.at[1]),
    )
    mixed_ref[...] = (hidden * gated_ref[...]).astype(jnp.bfloat16)
    for copy in copies:
        copy.wait()

    @pl.loop(0, steps)
    def _(j):
        at = pl.ds(pl.multiple_of(j * tn, tn), tn)
        full = bdot(mixed_ref[...], w_s[j])

        def body(odd):
            keep_ref[:, at] = full[odd * half : odd * half + half]
            send_ref[:, at] = full[(1 - odd) * half : (1 - odd) * half + half]

        either(odd_ref, body)

    for copy in outs:
        copy.wait()


def mix(odd, state_in, prod, state, gated, w):
    rows, local_w = prod.shape
    width = w.shape[1]
    tn = 512
    vmem = pl.BlockSpec(memory_space=pltpu.VMEM)
    part = jax.ShapeDtypeStruct((rows // 2, width), jnp.float32)
    return pl.pallas_call(
        mix_kernel,
        in_specs=[pl.BlockSpec(memory_space=pltpu.SMEM)]
        + [vmem] * 4
        + [pl.BlockSpec(memory_space=pltpu.HBM)],
        out_specs=[vmem] * 3 + [pl.BlockSpec(memory_space=pltpu.HBM)] * 2,
        out_shape=(
            jax.ShapeDtypeStruct((rows, local_w), jnp.bfloat16),
            part, part,
            kept((rows, local_w), jnp.float32),
            kept((1, local_w), jnp.float32),
        ),
        scratch_shapes=[
            pltpu.VMEM((width // tn, local_w, tn), jnp.bfloat16),
            pltpu.SemaphoreType.DMA((width // tn,)),
            pltpu.VMEM((rows, local_w), jnp.float32),
            pltpu.SemaphoreType.DMA((2,)),
        ],
        cost_estimate=pl.CostEstimate(
            flops=2 * rows * local_w * width,
            bytes_accessed=2 * local_w * width + 4 * rows * width,
            transcendentals=0,
        ),
        compiler_params=pltpu.CompilerParams(vmem_limit_bytes=SMALL_VMEM),
        name="mix",
    )(odd, state_in, prod, state, gated, *in_hbm(w))


def ffn_act(normed, d_act, gw_ref, uw_ref, rest_ref):
    tn = gw_ref.shape[1]
    main = tn // 256 * 256
    rest = bdot(normed, rest_ref[...])
    gate = jnp.concatenate([bdot(normed, gw_ref[:, 0:main]), rest[:, 0 : tn - main]], axis=1)
    up = jnp.concatenate([bdot(normed, uw_ref[:, 0:main]), rest[:, tn - main :]], axis=1)
    gelu, slope = gelu_parts(gate)
    act = (gelu * up).astype(jnp.bfloat16)
    d_gate = (d_act * up * slope).astype(jnp.bfloat16)
    d_up = (d_act * gelu).astype(jnp.bfloat16)
    return act, d_gate, d_up


def fill_rest(gw_ref, uw_ref, rest_s):
    tn = gw_ref.shape[1]
    main = tn // 256 * 256
    rest_s[:, 0 : tn - main] = gw_ref[:, main:tn]
    rest_s[:, tn - main :] = uw_ref[:, main:tn]


def start_kernel(odd_ref, cot_ref, share_ref, x_ref, own_ref, share_out, tail_ref):
    own_ref[...] = cot_ref[...]
    share_out[...] = share_ref[...]
    tail_ref[...] = x_ref[...]


def start(odd, cot, x_low, share):
    rows, width = cot.shape
    half = rows // 2
    part = half // share
    return pl.pallas_call(
        start_kernel,
        grid_spec=pltpu.PrefetchScalarGridSpec(
            num_scalar_prefetch=1,
            grid=(1,),
            in_specs=[
                pl.BlockSpec((half, width), lambda i, odd_ref: (odd_ref[0], 0)),
                pl.BlockSpec((part, width), lambda i, odd_ref: (odd_ref[0] * share + odd_ref[2], 0)),
                pl.BlockSpec((8, width), lambda i, odd_ref: (rows // 8 - 1, 0)),
            ],
            out_specs=[
                pl.BlockSpec((half, width), lambda i, odd_ref: (0, 0)),
                pl.BlockSpec((part, width), lambda i, odd_ref: (0, 0)),
                pl.BlockSpec((8, width), lambda i, odd_ref: (0, 0)),
            ],
        ),
        out_shape=(
            kept((half, width), cot.dtype),
            kept((part, width), cot.dtype),
            jax.ShapeDtypeStruct((8, width), x_low.dtype),
        ),
        compiler_params=pltpu.CompilerParams(vmem_limit_bytes=SMALL_VMEM // 2),
        name="start",
    )(odd, *in_hbm(cot, cot, x_low))


def braid_kernel(odd_ref, own_ref, far_ref, out_ref):
    part = own_ref.shape[0]
    second = odd_ref[2]
    out_ref[pl.ds(pl.multiple_of(second * part, 8), part), :] = own_ref[...]
    out_ref[pl.ds(pl.multiple_of((1 - second) * part, 8), part), :] = far_ref[...]


def braid(odd, own, far, blocks):
    rows, width = own.shape
    part = rows // blocks
    side = pl.BlockSpec((part, width), lambda i, odd_ref: (i, 0))
    return pl.pallas_call(
        braid_kernel,
        grid_spec=pltpu.PrefetchScalarGridSpec(
            num_scalar_prefetch=1,
            grid=(blocks,),
            in_specs=[side, side],
            out_specs=pl.BlockSpec((2 * part, width), lambda i, odd_ref: (i, 0)),
        ),
        out_shape=jax.ShapeDtypeStruct((2 * rows, width), own.dtype),
        cost_estimate=pl.CostEstimate(
            flops=0, bytes_accessed=8 * rows * width, transcendentals=0
        ),
        compiler_params=pltpu.CompilerParams(vmem_limit_bytes=SMALL_VMEM // 2),
        name="braid",
    )(odd, *in_hbm(own, far))


def d_act_kernel(odd_ref, c_ref, dw_ref, out_ref):
    half = c_ref.shape[0] // 2
    full = dot_t(c_ref[...], dw_ref[...])

    def body(odd):
        out_ref[0:half, :] = full[odd * half : odd * half + half]
        out_ref[half:, :] = full[(1 - odd) * half : (1 - odd) * half + half]

    either(odd_ref, body)


def own_d_act(odd, cot, dw):
    rows, width = cot.shape
    half = rows // 2
    local_f = dw.shape[0]
    tn = 640
    whole = pl.BlockSpec((rows, width), lambda j: (0, 0))
    return pl.pallas_call(
        d_act_kernel,
        grid=(local_f // tn,),
        in_specs=[
            pl.BlockSpec(memory_space=pltpu.SMEM), whole,
            pl.BlockSpec((tn, width), lambda j: (j, 0)),
        ],
        out_specs=pl.BlockSpec((2 * half, tn), lambda j: (0, j)),
        out_shape=jax.ShapeDtypeStruct((2 * half, local_f), jnp.float32),
        cost_estimate=pl.CostEstimate(
            flops=4 * half * width * local_f,
            bytes_accessed=2 * width * local_f,
            transcendentals=0,
        ),
        compiler_params=pltpu.CompilerParams(vmem_limit_bytes=SMALL_VMEM),
        name="own_d_act",
    )(odd, *in_hbm(cot, dw))


def ffn_own_kernel(
    nfar_ref, da_ref, n_hbm, gw_hbm, uw_hbm, keep_ref, send_ref, act_ref,
    n_s, rest_s, gw_s, uw_s, sems, n_sem,
):
    half = keep_ref.shape[0]
    steps, _, tn = gw_s.shape
    main = tn // 256 * 256
    (n_copy,) = begin(pltpu.make_async_copy(n_hbm, n_s.at[0:half, :], n_sem.at[0]))
    for j in range(steps):
        at = slice(j * tn, (j + 1) * tn)
        begin(
            pltpu.make_async_copy(gw_hbm.at[:, at], gw_s.at[j], sems.at[0, j]),
            pltpu.make_async_copy(uw_hbm.at[:, at], uw_s.at[j], sems.at[1, j]),
        )
    n_s[half:, :] = nfar_ref[...]
    keep_ref[...] = jnp.zeros_like(keep_ref)
    send_ref[...] = jnp.zeros_like(send_ref)
    n_copy.wait()

    @pl.loop(0, steps)
    def _(j):
        at = pl.ds(pl.multiple_of(j * tn, tn), tn)
        gw_ref, uw_ref = gw_s.at[j], uw_s.at[j]
        pltpu.make_async_copy(gw_hbm.at[:, at], gw_ref, sems.at[0, j]).wait()
        pltpu.make_async_copy(uw_hbm.at[:, at], uw_ref, sems.at[1, j]).wait()
        fill_rest(gw_ref, uw_ref, rest_s)
        act, d_gate, d_up = ffn_act(n_s[...], da_ref[:, at], gw_ref, uw_ref, rest_s)
        act_ref[:, at] = act
        d_rest = jnp.concatenate([d_gate[:, main:], d_up[:, main:]], axis=1)
        d_n = dot_t(d_gate[:, 0:main], gw_ref[:, 0:main])
        d_n = d_n + dot_t(d_up[:, 0:main], uw_ref[:, 0:main])
        d_n = d_n + dot_t(d_rest, rest_s[...])
        keep_ref[...] += d_n[0:half]
        send_ref[...] += d_n[half:]


def ffn_own(normed, normed_far, d_act, gw, uw):
    half, width = normed.shape
    rows = 2 * half
    local_f = gw.shape[1]
    tn = 640
    steps = local_f // tn
    vmem = pl.BlockSpec(memory_space=pltpu.VMEM)
    hbm = pl.BlockSpec(memory_space=pltpu.HBM)
    part = jax.ShapeDtypeStruct((half, width), jnp.float32)
    return pl.pallas_call(
        ffn_own_kernel,
        in_specs=[vmem] * 2 + [hbm] * 3,
        out_specs=[vmem] * 3,
        out_shape=(part, part, jax.ShapeDtypeStruct((rows, local_f), jnp.bfloat16)),
        scratch_shapes=[
            pltpu.VMEM((rows, width), jnp.bfloat16),
            pltpu.VMEM((width, 2 * (tn % 256)), jnp.bfloat16),
            pltpu.VMEM((steps, width, tn), jnp.bfloat16),
            pltpu.VMEM((steps, width, tn), jnp.bfloat16),
            pltpu.SemaphoreType.DMA((2, steps)),
            pltpu.SemaphoreType.DMA((1,)),
        ],
        cost_estimate=pl.CostEstimate(
            flops=8 * rows * width * local_f,
            bytes_accessed=4 * width * local_f,
            transcendentals=rows * local_f,
        ),
        compiler_params=pltpu.CompilerParams(vmem_limit_bytes=36 * MIB),
        name="ffn_own",
    )(normed_far, d_act, *in_hbm(normed, gw, uw))


def ffn_out_kernel(act_ref, dw_ref, keep_ref, send_ref):
    half = keep_ref.shape[0]
    out = bdot(act_ref[...], dw_ref[...])
    keep_ref[...] = out[0:half]
    send_ref[...] = out[half:]


def ffn_out(act, dw):
    rows, local_f = act.shape
    width = dw.shape[1]
    tn = 512
    part = pl.BlockSpec((rows // 2, tn), lambda j: (0, j))
    shape = jax.ShapeDtypeStruct((rows // 2, width), jnp.float32)
    return pl.pallas_call(
        ffn_out_kernel,
        grid=(width // tn,),
        in_specs=[
            pl.BlockSpec((rows, local_f), lambda j: (0, 0)),
            pl.BlockSpec((local_f, tn), lambda j: (0, j)),
        ],
        out_specs=[part, part],
        out_shape=(shape, shape),
        cost_estimate=pl.CostEstimate(
            flops=2 * rows * width * local_f,
            bytes_accessed=2 * width * local_f,
            transcendentals=0,
        ),
        compiler_params=pltpu.CompilerParams(vmem_limit_bytes=SMALL_VMEM),
        name="ffn_out",
    )(act, *in_hbm(dw))


def ffn_all_kernel(
    sub, span, place_ref, n_ref, nfar_ref, c_ref, cfar_ref, gw_ref, uw_ref, dw_ref,
    gg_ref, gu_ref, gd_ref, both, act_s, rest_s, nt_s, ct_s,
):
    rows = n_ref.shape[0]
    tn = gw_ref.shape[1]
    cols = gg_ref.shape[0]
    chunk = pl.program_id(1)
    fill_rest(gw_ref, uw_ref, rest_s)

    @pl.when(pl.program_id(0) == 0)
    def _():
        start = place_ref[1] * cols
        width = n_ref.shape[1]
        base = pl.multiple_of(jnp.minimum(start // 128 * 128, width - span), 128)
        row = lax.broadcasted_iota(jnp.int32, (cols, span), 0)
        col = lax.broadcasted_iota(jnp.int32, (cols, span), 1)
        pick = jnp.where(col == row + (start - base), 1.0, 0.0).astype(jnp.bfloat16)
        for to, pair in ((nt_s, (n_ref, nfar_ref)), (ct_s, (c_ref, cfar_ref))):
            for k, ref in enumerate(pair):
                turned_cols = dot_t(pick, ref[:, pl.ds(base, span)])
                to[chunk, :, k * rows : (k + 1) * rows] = turned_cols.astype(jnp.bfloat16)

    for base, n, c in ((0, n_ref, c_ref), (rows, nfar_ref, cfar_ref)):
        for i in range(0, rows, sub):
            to = slice(base + i, base + i + sub)
            d_act = dot_t(c[i : i + sub, :], dw_ref[...])
            act, d_gate, d_up = ffn_act(n[i : i + sub, :], d_act, gw_ref, uw_ref, rest_s)
            act_s[to, :] = act
            both[to, 0:tn] = d_gate
            both[to, tn : 2 * tn] = d_up

    grads = bdot(nt_s[chunk], both[...])
    down = bdot(ct_s[chunk], act_s[...])
    first = pl.program_id(1) == 0

    @pl.when(first)
    def _():
        gg_ref[...] = grads[:, 0:tn]
        gu_ref[...] = grads[:, tn:]
        gd_ref[...] = down

    @pl.when(jnp.logical_not(first))
    def _():
        gg_ref[...] += grads[:, 0:tn]
        gu_ref[...] += grads[:, tn:]
        gd_ref[...] += down


def ffn_all(place, cols, normed, normed_far, cot, cot_far, gw, uw, dw):
    rows, width = cot.shape
    local_f = gw.shape[1]
    skip = max(k * cols % 128 for k in range(width // cols))
    span = -(-(cols + skip) // 128) * 128
    tn = 640
    sub = 320
    chunk = rows if rows <= 640 else sub
    once = pl.Buffered(1) if chunk == rows else pl.Buffered(2)
    tall = pl.BlockSpec((chunk, width), lambda j, r: (r, 0), pipeline_mode=once)
    col = pl.BlockSpec((width, tn), lambda j, r: (0, j))
    out_col = pl.BlockSpec((cols, tn), lambda j, r: (0, j))
    wide = jax.ShapeDtypeStruct((cols, local_f), jnp.float32)
    return pl.pallas_call(
        functools.partial(ffn_all_kernel, sub, span),
        grid=(local_f // tn, rows // chunk),
        in_specs=[pl.BlockSpec(memory_space=pltpu.SMEM)]
        + [tall] * 4
        + [col, col, pl.BlockSpec((tn, width), lambda j, r: (j, 0))],
        out_specs=[out_col] * 3,
        out_shape=(wide,) * 3,
        scratch_shapes=[
            pltpu.VMEM((2 * chunk, 2 * tn), jnp.bfloat16),
            pltpu.VMEM((2 * chunk, tn), jnp.bfloat16),
            pltpu.VMEM((width, 2 * (tn % 256)), jnp.bfloat16),
            pltpu.VMEM((rows // chunk, cols, 2 * chunk), jnp.bfloat16),
            pltpu.VMEM((rows // chunk, cols, 2 * chunk), jnp.bfloat16),
        ],
        cost_estimate=pl.CostEstimate(
            flops=12 * rows * width * local_f + 12 * rows * cols * local_f,
            bytes_accessed=6 * width * local_f + 8 * rows * width + 12 * cols * local_f,
            transcendentals=2 * rows * local_f,
        ),
        compiler_params=pltpu.CompilerParams(vmem_limit_bytes=58 * 1024 * 1024),
        name="ffn_all",
    )(place, normed, normed_far, cot, cot_far, gw, uw, dw)


def sums_kernel(cols, half, packed_ref, gx_ref, ga_ref, vec_ref, gain_ref):
    blocks, _, span = packed_ref.shape
    total = packed_ref[0, half:, :].astype(jnp.float32)
    for k in range(1, blocks):
        total = total + packed_ref[k, half:, :].astype(jnp.float32)
    tall, local_w = gx_ref.shape
    pieces = local_w // span
    for g, ref in enumerate((gx_ref, ga_ref)):
        for q in range(pieces):
            at = (g * pieces + q) * tall
            ref[:, q * span : (q + 1) * span] = total[at : at + tall]
    small = total[2 * pieces * tall :]
    thin = vec_ref.shape[1]
    vec_ref[...] = small[:, 0:thin] + small[:, cols : cols + thin]
    gain_ref[...] = jnp.broadcast_to(small[6:7] + small[7:8], gain_ref.shape)


def token_grads_kernel(
    half, odd_ref, mixed_ref, mfar_ref, b_ref, bfar_ref, own_ref, far_ref, out_ref, y_ref, x_ref
):
    rows, local_w = mixed_ref.shape
    span = own_ref.shape[2]
    cols = span // 2
    out = both = None
    for m, b, p in ((mixed_ref, b_ref, own_ref), (mfar_ref, bfar_ref, far_ref)):
        side = p[:, 0:half, :].reshape(rows, span)
        term = tdot(side[:, cols:], m[...])
        out = term if out is None else out + term
        term = tdot(side[:, 0:cols], b[...])
        both = term if both is None else both + term
    out_ref[...] = out
    y_ref[...] = both[:, 0:local_w]
    x_ref[...] = both[:, local_w:]


def token_grads(odd, gathered, first, branches, packed, packed_far, half, local_w):
    rows = gathered.shape[0]
    span = packed.shape[2]
    cols = span // 2
    window = lambda tile, at, flip: pl.BlockSpec(
        (rows, tile), lambda i, odd_ref: (0, at + (1 - odd_ref[0] if flip else odd_ref[0]))
    )
    whole = pl.BlockSpec(packed.shape, lambda i, odd_ref: (0, 0, 0))
    out = pl.BlockSpec((cols, local_w), lambda i, odd_ref: (0, 0))
    return pl.pallas_call(
        functools.partial(token_grads_kernel, half),
        grid_spec=pltpu.PrefetchScalarGridSpec(
            num_scalar_prefetch=1,
            grid=(1,),
            in_specs=[
                window(local_w, first, False), window(local_w, first, True),
                window(2 * local_w, 0, False), window(2 * local_w, 0, True), whole, whole,
            ],
            out_specs=[out] * 3,
        ),
        out_shape=(jax.ShapeDtypeStruct((cols, local_w), jnp.float32),) * 3,
        cost_estimate=pl.CostEstimate(
            flops=12 * rows * cols * local_w, bytes_accessed=16 * rows * local_w, transcendentals=0
        ),
        compiler_params=pltpu.CompilerParams(vmem_limit_bytes=58 * MIB),
        name="token_grads",
    )(odd, *in_hbm(gathered, gathered, branches, branches, packed, packed_far))


def back_kernel(
    odd_ref, own_ref, far_ref, hidden_ref, gated_ref, slope_ref, decay_ref, prod_ref, w_hbm,
    dy_ref, lam_ref, after_ref, total_ref, acc, d_s, w_s, sems,
):
    half = own_ref.shape[0]
    rows = 2 * half
    steps, _, tk = w_s.shape
    copies = begin(
        *[
            pltpu.make_async_copy(w_hbm.at[:, j * tk : (j + 1) * tk], w_s.at[j], sems.at[j])
            for j in range(steps)
        ]
    )
    d_s[0:half, :] = own_ref[...]
    d_s[half:, :] = far_ref[...]
    acc[...] = jnp.zeros_like(acc)
    for copy in copies:
        copy.wait()

    @pl.loop(0, steps)
    def _(j):
        acc[...] += dot_t(d_s[:, pl.ds(pl.multiple_of(j * tk, tk), tk)], w_s[j])

    def body(odd):
        for to, at in ((odd * half, 0), ((1 - odd) * half, half)):
            rows_to = slice(to, to + half)
            d_mixed = acc[at : at + half, :]
            dy_ref[rows_to, :] = (
                d_mixed * hidden_ref[rows_to, :] * slope_ref[rows_to, :]
            ).astype(jnp.bfloat16)
            lam_ref[rows_to, :] = d_mixed * gated_ref[rows_to, :]

    either(odd_ref, body)

    def next_decay(at):
        if at + 8 < rows:
            return decay_ref[at + 1 : at + 9, :]
        last = pltpu.roll(decay_ref[at : at + 8, :], 7, 0)
        row = lax.broadcasted_iota(jnp.int32, last.shape, 0)
        return jnp.where(row == 7, 1.0, last)

    def store(at, p, h):
        after_ref[at : at + 8, :] = p
        lam_ref[at : at + 8, :] = h

    _, first = scan_rows(True, next_decay, lambda at: lam_ref[at : at + 8, :], rows, store)
    total_ref[0:1, :] = prod_ref[0:1, :]
    total_ref[1:2, :] = decay_ref[0:1, :] * first


def back(odd, own, far, w, hidden, gated, slope, decay, prod):
    half, width = own.shape
    rows = 2 * half
    local_w = w.shape[0]
    tk = 512
    vmem = pl.BlockSpec(memory_space=pltpu.VMEM)
    wide = jax.ShapeDtypeStruct((rows, local_w), jnp.float32)
    return pl.pallas_call(
        back_kernel,
        in_specs=[pl.BlockSpec(memory_space=pltpu.SMEM)]
        + [vmem] * 7
        + [pl.BlockSpec(memory_space=pltpu.HBM)],
        out_specs=[vmem] * 4,
        out_shape=(
            jax.ShapeDtypeStruct((rows, local_w), jnp.bfloat16), wide, wide,
            jax.ShapeDtypeStruct((2, local_w), jnp.float32),
        ),
        scratch_shapes=[
            pltpu.VMEM((rows, local_w), jnp.float32),
            pltpu.VMEM((rows, width), jnp.bfloat16),
            pltpu.VMEM((width // tk, local_w, tk), jnp.bfloat16),
            pltpu.SemaphoreType.DMA((width // tk,)),
        ],
        cost_estimate=pl.CostEstimate(
            flops=2 * rows * width * local_w,
            bytes_accessed=2 * width * local_w + 30 * rows * local_w,
            transcendentals=0,
        ),
        compiler_params=pltpu.CompilerParams(vmem_limit_bytes=SMALL_VMEM),
        name="back",
    )(odd, own, far, hidden, gated, slope, decay, prod, *in_hbm(w))


def gates_back_kernel(
    odd_ref, returned_ref, state_in_ref, lam_ref, after_ref, hidden_ref, decay_ref, mult_ref,
    conv_ref, low_ref, far_ref, gx_ref, ga_ref, wx_ref, wa_ref, soft_ref, sig_ref,
    dconv_ref, dfar_ref, halo_ref, gwx_ref, gwa_ref, gdecay_ref, dgx_s, dga_s,
):
    _, local_w = conv_ref.shape
    head = wx_ref.shape[0]
    lam = lam_ref[...] + after_ref[...] * returned_ref[...]
    decay, mult, gx, ga = decay_ref[...], mult_ref[...], gx_ref[...], ga_ref[...]
    conv = conv_ref[...]
    before = pltpu.roll(hidden_ref[...], 1, 0)
    row = lax.broadcasted_iota(jnp.int32, before.shape, 0)
    before = jnp.where(row == 0, state_in_ref[...], before)
    lam_gx = lam * gx
    d_log = lam * before * decay - lam_gx * conv * decay * decay / mult
    scaled = d_log * -8.0 * ga
    gdecay_ref[...] = jnp.sum(scaled, axis=0, keepdims=True) * sig_ref[...]
    dga_s[...] = (scaled * soft_ref[...] * (1.0 - ga)).astype(jnp.bfloat16)
    lam_gx_m = lam_gx * mult
    dgx_s[...] = (lam_gx_m * conv * (1.0 - gx)).astype(jnp.bfloat16)
    dconv_ref[...] = lam_gx_m

    def body(odd):
        src = {"own": low_ref, "far": far_ref}
        for lo, hi, parts in head_blocks(odd, local_w, head):
            d_x, d_a = dgx_s[:, lo:hi], dga_s[:, lo:hi]
            for r0, r1, name, s0, s1 in parts:
                piece = src[name][:, s0:s1]
                gwx_ref[r0:r1, lo:hi] = tdot(piece, d_x)
                gwa_ref[r0:r1, lo:hi] = tdot(piece, d_a)
                term = dot_t(d_x, wx_ref[r0:r1, lo:hi]) + dot_t(d_a, wa_ref[r0:r1, lo:hi])
                if name == "own":
                    dconv_ref[:, s0:s1] += term
                else:
                    dfar_ref[...] = term

    either(odd_ref, body)
    halo_ref[:, 0:local_w] = dconv_ref[0:8, :]
    halo_ref[:, local_w:] = dfar_ref[0:8, :]


def gates_back(odd, returned, state_in, lam, after, hidden, decay, mult, conv, low, far, gx, ga, wx, wa, soft, sig):
    rows, local_w = conv.shape
    head = wx.shape[0]
    f32 = jnp.float32
    vmem = pl.BlockSpec(memory_space=pltpu.VMEM)
    return pl.pallas_call(
        gates_back_kernel,
        in_specs=[pl.BlockSpec(memory_space=pltpu.SMEM)] + [vmem] * 16,
        out_specs=[vmem] * 6,
        out_shape=(
            jax.ShapeDtypeStruct((rows, local_w), f32),
            jax.ShapeDtypeStruct((rows, local_w % head), f32),
            jax.ShapeDtypeStruct((8, local_w + local_w % head), f32),
            jax.ShapeDtypeStruct((head, local_w), f32),
            jax.ShapeDtypeStruct((head, local_w), f32),
            jax.ShapeDtypeStruct((1, local_w), f32),
        ),
        scratch_shapes=[pltpu.VMEM((rows, local_w), jnp.bfloat16)] * 2,
        cost_estimate=pl.CostEstimate(
            flops=8 * rows * head * local_w + 40 * rows * local_w,
            bytes_accessed=44 * rows * local_w,
            transcendentals=rows * local_w,
        ),
        compiler_params=pltpu.CompilerParams(vmem_limit_bytes=SMALL_VMEM),
        name="gates_back",
    )(odd, returned, state_in, lam, after, hidden, decay, mult, conv, low, far, gx, ga, wx, wa, soft, sig)


def tail_kernel(
    odd_ref, dconv_ref, far_ref, later_ref, dy_ref, gdecay_ref, pad_hbm, cw_hbm, r_hbm, xw_hbm,
    yw_hbm, x_hbm, keep_ref, send_ref, branch_ref, vec_ref, mix_ref,
    ext, dx_s, pad_ref, cw_ref, r_ref, xw_s, yw_s, x_s, sems,
):
    rows, local_w = dconv_ref.shape
    rest = far_ref.shape[1]
    half = rows // 2
    steps, tn, _ = xw_s.shape
    copy = pltpu.make_async_copy
    early = begin(
        copy(pad_hbm, pad_ref, sems.at[0]), copy(cw_hbm, cw_ref, sems.at[1]),
        copy(r_hbm, r_ref, sems.at[2]),
    )
    weights = []
    for j in range(steps):
        at = slice(j * tn, (j + 1) * tn)
        weights += begin(
            copy(xw_hbm.at[at, :], xw_s.at[j], sems.at[3 + 3 * j]),
            copy(yw_hbm.at[at, :], yw_s.at[j], sems.at[4 + 3 * j]),
            copy(x_hbm.at[:, at], x_s.at[j], sems.at[5 + 3 * j]),
        )
    ext[0:rows, :] = dconv_ref[...]
    ext[rows : rows + 8, :] = later_ref[:, 0:local_w]

    def body(odd):
        lo = 0 if odd else local_w - rest
        ext[:, lo : lo + rest] += far_ref[...]

    either(odd_ref, body)
    for part in early:
        part.wait()
    d_conv = ext[0:rows, :]
    vec_ref[4:5, :] = jnp.sum(d_conv, axis=0, keepdims=True)
    vec_ref[5:6, :] = gdecay_ref[...]
    vec_ref[6:8, :] = jnp.zeros((2, local_w), jnp.float32)
    d_x = cw_ref[3:4, :] * d_conv
    for offset in range(4):
        shifted_in = pad_ref[5 + offset : 5 + offset + rows, :]
        vec_ref[offset : offset + 1, :] = jnp.sum(d_conv * shifted_in, axis=0, keepdims=True)
        if offset < 3:
            d_x = d_x + cw_ref[offset : offset + 1, :] * ext[3 - offset : 3 - offset + rows, :]
    dx_s[...] = d_x.astype(jnp.bfloat16)
    for k in (0, 1):
        rows_k = slice(k * half, (k + 1) * half)
        branch_ref[:, 2 * k * local_w : (2 * k + 1) * local_w] = dy_ref[rows_k, :]
        branch_ref[:, (2 * k + 1) * local_w : (2 * k + 2) * local_w] = dx_s[rows_k, :]
    for part in weights:
        part.wait()

    @pl.loop(0, steps)
    def _(j):
        at = pl.ds(pl.multiple_of(j * tn, tn), tn)
        full = dot_t(dx_s[...], xw_s[j]) + dot_t(dy_ref[...], yw_s[j])
        n_one = x_s[j].astype(jnp.float32) * r_ref[...]
        mix_ref[:, at] = jnp.sum(full * n_one, axis=0, keepdims=True)

        def split(odd):
            keep_ref[:, at] = full[odd * half : odd * half + half]
            send_ref[:, at] = full[(1 - odd) * half : (1 - odd) * half + half]

        either(odd_ref, split)


def tail(odd, dconv, far, later, pad, cw, dy, gdecay, xw, yw, x_low, r_one):
    rows, local_w = dconv.shape
    width = xw.shape[0]
    tn = 512
    steps = width // tn
    f32, bf16 = jnp.float32, jnp.bfloat16
    vmem = pl.BlockSpec(memory_space=pltpu.VMEM)
    hbm = pl.BlockSpec(memory_space=pltpu.HBM)
    part = jax.ShapeDtypeStruct((rows // 2, width), f32)
    return pl.pallas_call(
        tail_kernel,
        in_specs=[pl.BlockSpec(memory_space=pltpu.SMEM)] + [vmem] * 5 + [hbm] * 6,
        out_specs=[vmem] * 5,
        out_shape=(
            part, part,
            jax.ShapeDtypeStruct((rows // 2, 4 * local_w), bf16),
            jax.ShapeDtypeStruct((8, local_w), f32),
            jax.ShapeDtypeStruct((1, width), f32),
        ),
        scratch_shapes=[
            pltpu.VMEM((rows + 8, local_w), f32),
            pltpu.VMEM((rows, local_w), bf16),
            pltpu.VMEM((rows + 8, local_w), f32),
            pltpu.VMEM((4, local_w), f32),
            pltpu.VMEM((rows, 1), f32),
            pltpu.VMEM((steps, tn, local_w), bf16),
            pltpu.VMEM((steps, tn, local_w), bf16),
            pltpu.VMEM((steps, rows, tn), bf16),
            pltpu.SemaphoreType.DMA((3 + 3 * steps,)),
        ],
        cost_estimate=pl.CostEstimate(
            flops=4 * rows * local_w * width,
            bytes_accessed=4 * local_w * width + 8 * rows * width,
            transcendentals=0,
        ),
        compiler_params=pltpu.CompilerParams(vmem_limit_bytes=SMALL_VMEM),
        name="tail",
    )(odd, dconv, far, later, dy, gdecay, *in_hbm(pad, cw, r_one, xw, yw, x_low))


def join_kernel(first, last, at, reverse, flag_ref, total_ref, other_ref, *refs):
    before_ref = None if first else refs[0]
    outs = refs if first else refs[1:]
    own_a, own_b = total_ref[0:1, :], total_ref[1:2, :]
    far_a, far_b = other_ref[0:1, :], other_ref[1:2, :]
    upper = jnp.full(own_a.shape, flag_ref[at], jnp.int32)
    far_first = upper == (0 if reverse else 1)
    if first:
        new_a = jnp.where(far_first, far_a, 1.0)
        new_b = jnp.where(far_first, far_b, 0.0)
    else:
        old_a, old_b = before_ref[0:1, :], before_ref[1:2, :]
        new_a = jnp.where(far_first, far_a * old_a, old_a)
        new_b = jnp.where(far_first, old_a * far_b + old_b, old_b)
    if last:
        outs[0][...] = new_b
        return
    outs[0][0:1, :] = new_a
    outs[0][1:2, :] = new_b
    outs[1][0:1, :] = own_a * far_a
    outs[1][1:2, :] = jnp.where(far_first, own_a * far_b + own_b, far_a * own_b + far_b)


def carried(odd, total, reverse):
    size = lax.axis_size("seq")
    pair = (total.shape, jnp.float32)
    before = None
    bit, at = 1, 3
    while bit < size:
        other = swap(total, "seq", bit)
        last = 2 * bit >= size
        args = (total, other) if before is None else (total, other, before)
        outs = [((1, total.shape[1]), jnp.float32)] if last else [pair, pair]
        kernel = functools.partial(join_kernel, before is None, last, at, reverse)
        joined = small_call(kernel, outs, (odd,), *args)
        before, total = (joined[0], None) if last else joined
        bit, at = 2 * bit, at + 1
    return before


def low_kernel(keep_ref, far_ref, low_ref):
    low_ref[...] = (keep_ref[...] + far_ref[...]).astype(jnp.bfloat16)


def low_sum_kernel(low_ref, far_ref, out_ref):
    out_ref[...] = (
        low_ref[...].astype(jnp.float32) + far_ref[...].astype(jnp.float32)
    ).astype(jnp.bfloat16)


def pair_sum(keep, send):
    far = swap(send, "mp", 1)
    bf16 = [(keep.shape, jnp.bfloat16)]
    (low,) = small_call(low_kernel, bf16, (), keep, far)
    bit = 2
    while True:
        far = swap(low, "mp", bit)
        bit *= 2
        if bit >= lax.axis_size("mp"):
            return low, far
        (low,) = small_call(low_sum_kernel, bf16, (), low, far)


def total_of(low_ref, far_ref):
    return low_ref[...].astype(jnp.float32) + far_ref[...].astype(jnp.float32)


def norm_two_kernel(
    odd_ref, x_ref, low_ref, far_ref, gain_ref, mixed_ref, x_one_ref, n_ref, r_ref, own_ref, out_ref
):
    half, width = low_ref.shape
    local_w = mixed_ref.shape[1]
    x_one = x_ref[...].astype(jnp.float32) + total_of(low_ref, far_ref)
    r = lax.rsqrt(jnp.mean(x_one * x_one, axis=-1, keepdims=True) + EPS)
    n = x_one * r
    normed = (n * gain_ref[...].reshape(1, width)).astype(jnp.bfloat16)
    x_one_ref[...] = x_one
    n_ref[...] = n
    r_ref[...] = r
    own_ref[...] = normed
    out_ref[:, 0:width] = normed
    out_ref[:, width : width + local_w] = mixed_ref[0:half, :]
    out_ref[:, width + local_w :] = mixed_ref[half:, :]


def d_x_kernel(
    odd_ref, low_ref, far_ref, gain_ref, n_ref, r_ref, cot_ref, d_x_ref, d_low_ref, g_ref
):
    d_n = total_of(low_ref, far_ref)
    n = n_ref[...]
    g_ref[...] = jnp.sum(d_n * n, axis=0, keepdims=True)
    e = gain_ref[...].reshape(1, n.shape[1]) * d_n
    mean = jnp.mean(e * n, axis=-1, keepdims=True)
    d_x = cot_ref[...].astype(jnp.float32) + r_ref[...] * (e - n * mean)
    d_x_ref[...] = d_x
    d_low_ref[...] = d_x.astype(jnp.bfloat16)


def far_kernel(far_ref, later_ref, out_ref):
    rows, rest = far_ref.shape
    out_ref[0:rows, :] = far_ref[...]
    out_ref[rows:, :] = later_ref[:, later_ref.shape[1] - rest :]


def pack_kernel(
    odd_ref, normed_ref, gx_ref, ga_ref, vec_ref, mix_ref, d_x_ref, ffn_ref, out_ref
):
    blocks, _, span = out_ref.shape
    half = normed_ref.shape[0]
    cols = span // 2
    head, local_w = gx_ref.shape
    tall = head // blocks
    pieces = local_w // span
    bf16 = jnp.bfloat16

    def parts(value):
        high = value.astype(bf16)
        return high, (value - high.astype(jnp.float32)).astype(bf16)

    out_ref[:, half + 2 * tall * pieces :, :] = jnp.zeros((blocks, 8, span), bf16)
    thin = local_w // blocks
    for s in range(blocks):
        out_ref[s, 0:half, 0:cols] = normed_ref[:, s * cols : (s + 1) * cols]
        out_ref[s, 0:half, cols:] = d_x_ref[:, s * cols : (s + 1) * cols]
        for g, ref in enumerate((gx_ref, ga_ref)):
            for q in range(pieces):
                at = half + (g * pieces + q) * tall
                out_ref[s, at : at + tall, :] = ref[
                    s * tall : (s + 1) * tall, q * span : (q + 1) * span
                ].astype(bf16)
        at = half + 2 * tall * pieces
        both = jnp.concatenate(
            [ffn_ref[:, s * cols : (s + 1) * cols], mix_ref[:, s * cols : (s + 1) * cols]], axis=1
        )
        row = lax.broadcasted_iota(jnp.int32, (8, span), 0)
        high, rest = parts(both)
        lines = jnp.where(row == 6, high.astype(jnp.float32), rest.astype(jnp.float32))
        out_ref[s, at : at + 8, :] = jnp.where(row < 6, 0.0, lines).astype(bf16)
        high, rest = parts(vec_ref[0:6, s * thin : (s + 1) * thin])
        out_ref[s, at : at + 6, 0:thin] = high
        out_ref[s, at : at + 6, cols : cols + thin] = rest


def last_kernel(
    odd_ref, x_ref, r_ref, low_ref, far_ref, gain_ref, d_x_ref, out_ref
):
    d_n = total_of(low_ref, far_ref)
    r = r_ref[...]
    n = x_ref[...].astype(jnp.float32) * r
    e = gain_ref[...].reshape(1, n.shape[1]) * d_n
    mean = jnp.mean(e * n, axis=-1, keepdims=True)
    out_ref[...] = (d_x_ref[...] + r * (e - n * mean)).astype(jnp.bfloat16)


def out_own_kernel(odd_ref, low_ref, far_ref, x_one_ref, out_ref):
    out_ref[...] = (x_one_ref[...] + total_of(low_ref, far_ref)).astype(jnp.bfloat16)


def order_kernel(odd_ref, own_ref, far_ref, out_ref):
    half = own_ref.shape[0]

    def body(odd):
        out_ref[odd * half : (odd + 1) * half, :] = own_ref[...]
        out_ref[(1 - odd) * half : (2 - odd) * half, :] = far_ref[...]

    either(odd_ref, body)


def per_device(
    block_input,
    mix_gain,
    x_weight,
    y_weight,
    conv_weight,
    conv_bias,
    input_gate,
    decay_gate,
    decay_param,
    out_weight,
    ffn_gain,
    gate_weight,
    up_weight,
    down_weight,
    out_cotangent,
):
    seq_count, rows, width = block_input.shape
    local_w = x_weight.shape[1]
    head = input_gate.shape[0]
    rest = local_w % head
    blocks = lax.axis_size("seq")
    place = lax.axis_index("seq").astype(jnp.int32)
    bits = [(place >> k) & 1 for k in range(max(1, (blocks - 1).bit_length()))]
    along = lax.axis_index("mp").astype(jnp.int32)
    odd = jnp.stack([along & 1, place, along >> 1] + bits)
    share = lax.axis_size("mp") // 2
    assert share == 2
    half = rows // 2
    cols = width // blocks
    bf16, f32 = jnp.bfloat16, jnp.float32
    half_wide = (half, width)

    x_low = block_input.reshape(rows, width)
    cot_low = out_cotangent.reshape(rows, width)

    cot_own, cot_part, tail_rows = start(odd, cot_low, x_low, share)
    cot_part = lax.all_gather(cot_part, "seq", axis=0, tiled=True)
    cot_across = swap(cot_part, "mp", 2)
    cot_mine = braid(odd, cot_part, cot_across, blocks)
    cot_far = swap(cot_mine, "mp", 1)

    inp_tail = shifted(tail_rows, "seq", 1)
    (
        conv_now, low_now, gated_now, far_out, soft_now,
        normed1, r_one, padded, y_slope, slope_sig, conv_out, conv_low, y_gated, softer,
    ) = front(
        odd, x_low, inp_tail, mix_gain, x_weight, y_weight, conv_weight, conv_bias, decay_param, rest
    )

    prod, local_state, total, gate_x, gate_a, decay, mult, far, block_total = gates(
        odd, conv_now, low_now, swap(far_out, "mp", 1), input_gate, decay_gate, soft_now
    )
    mixed, keep, send, hidden, state_in = mix(
        odd, carried(odd, total, False), prod, local_state, gated_now, out_weight
    )

    low, high = pair_sum(keep, send)
    d_act_own = own_d_act(odd, cot_low, down_weight)
    x_one, n_two, r_two, normed2_own, gather_in = half_call(
        norm_two_kernel, odd, (x_low,), (low, high, ffn_gain, mixed),
        [
            (half_wide, f32), (half_wide, f32), ((half, 1), f32), (half_wide, bf16),
            ((half, width + 2 * local_w), bf16),
        ],
    )
    normed2_far_own = swap(normed2_own, "mp", 1)
    normed2_mine = lax.all_gather(gather_in, "seq", axis=0, tiled=True)
    normed2_far = swap(normed2_mine, "mp", 1)

    keep, send, act_own = ffn_own(
        normed2_own, normed2_far_own, d_act_own, gate_weight, up_weight
    )
    low, high = pair_sum(keep, send)
    out_keep, out_send = ffn_out(act_own, down_weight)
    d_x_one, d_x_low, g_ffn_gain = half_call(
        d_x_kernel, odd, (), (low, high, ffn_gain),
        [(half_wide, f32), (half_wide, bf16), ((1, width), f32)], (n_two, r_two, cot_own),
    )

    d_y_low, local_lam, after_prod, total = back(
        odd, d_x_low, swap(d_x_low, "mp", 1), out_weight, hidden, y_gated, y_slope, decay, block_total
    )
    low, high = pair_sum(out_keep, out_send)
    (out_own,) = half_call(out_own_kernel, odd, (), (low, high), [(half_wide, bf16)], (x_one,))
    out_far = swap(out_own, "mp", 1)
    returned = carried(odd, total, True)
    d_conv, d_far, halo, g_input, g_decay_gate, g_decay = gates_back(
        odd, returned, state_in, local_lam, after_prod, hidden, decay, mult, conv_out, conv_low,
        far, gate_x, gate_a, input_gate, decay_gate, softer, slope_sig,
    )
    later = shifted(halo, "seq", -1)
    (far_out,) = small_call(far_kernel, [((rows + 8, rest), f32)], (), d_far, later)
    keep, send, branch_in, vectors, g_mix_gain = tail(
        odd, d_conv, swap(far_out, "mp", 1), later, padded, conv_weight, d_y_low, g_decay,
        x_weight, y_weight, x_low, r_one,
    )
    branches = lax.all_gather(branch_in, "seq", axis=0, tiled=True)
    low, high = pair_sum(keep, send)

    span = 2 * cols
    gate_rows = 2 * head // blocks * (local_w // span)
    (packed,) = half_call(
        pack_kernel, odd, (normed1,),
        (g_input, g_decay_gate, vectors, g_mix_gain),
        [((blocks, half + gate_rows + 8, span), bf16)], (d_x_low, g_ffn_gain),
    )
    packed = lax.all_to_all(packed, "seq", split_axis=0, concat_axis=0, tiled=True)
    g_gate, g_up, g_down = ffn_all(
        odd, cols, normed2_mine, normed2_far, cot_mine, cot_far,
        gate_weight, up_weight, down_weight,
    )
    packed, g_gate = lax.optimization_barrier((packed, g_gate))
    (in_own,) = half_call(
        last_kernel, odd, (x_low, r_one), (low, high, mix_gain),
        [(half_wide, bf16)], (d_x_one,),
    )
    order = lambda own, far: small_call(order_kernel, [((rows, width), bf16)], (odd,), own, far)[0]
    input_grad = order(in_own, swap(in_own, "mp", 1))
    block_output = order(out_own, out_far)

    packed_far = swap(packed, "mp", 1)
    g_in, g_dec, small, gains = small_call(
        functools.partial(sums_kernel, cols, half),
        [
            ((head // blocks, local_w), f32), ((head // blocks, local_w), f32),
            ((8, local_w // blocks), f32), ((8, span), f32),
        ],
        (), packed,
    )
    g_out, g_y, g_x = token_grads(
        odd, normed2_mine, width // local_w, branches, packed, packed_far, half, local_w
    )
    near = gains + swap(gains, "mp", 1)
    bit = 2
    wider = near
    while bit < lax.axis_size("mp"):
        wider = wider + swap(wider, "mp", bit)
        bit *= 2

    shape = (seq_count, rows, width)
    return (
        block_output.reshape(shape),
        input_grad.reshape(shape),
        wider[0, cols:],
        g_x,
        g_y,
        small[:4],
        small[4],
        g_in,
        g_dec,
        small[5],
        g_out.T,
        near[0, :cols],
        g_gate,
        g_up,
        g_down.T,
    )


def solution(mesh):
    in_specs = (
        P(None, "seq", None),
        P(),
        P(None, "mp"),
        P(None, "mp"),
        P(None, "mp"),
        P("mp"),
        P(None, "mp"),
        P(None, "mp"),
        P("mp"),
        P("mp", None),
        P(),
        P(None, "mp"),
        P(None, "mp"),
        P("mp", None),
        P(None, "seq", None),
    )
    out_specs = (
        P(None, "seq", None),
        P(None, "seq", None),
        P("seq"),
        P("seq", "mp"),
        P("seq", "mp"),
        P(None, ("mp", "seq")),
        P(("mp", "seq")),
        P("seq", "mp"),
        P("seq", "mp"),
        P(("mp", "seq")),
        P("mp", "seq"),
        P("seq"),
        P("seq", "mp"),
        P("seq", "mp"),
        P("mp", "seq"),
    )

    return jax.shard_map(
        per_device, mesh=mesh, in_specs=in_specs, out_specs=out_specs, check_vma=False
    )
```
